32 devices in a mesh: pipe: 8 (over y, x, core), tensor: 4 (over z).
Axes of the slice: x: 2, y: 2, z: 4, core: 2. Of those that a mesh axis runs over, the one named last changes fastest.
Arguments:
- section_inputs: bfloat16 [8, 2, 7168, 64], P('pipe', None, 'tensor'), may hold values from -6 to 6
- cotangent: bfloat16 [2, 7168, 64], P(None, 'tensor'), may hold values from -7 to 7
- documents: int32 [2, 64], replicated, may hold values from 0 to 3, never falling along the last dimension, each value on 1 to 32 neighbouring positions
- gain: float32 [8, 7168], P('pipe', 'tensor'), may hold values from 0.4 to 2
- w_query: bfloat16 [8, 7168, 256], P('pipe', 'tensor')
- w_key: bfloat16 [8, 7168, 256], P('pipe', 'tensor')
- w_value: bfloat16 [8, 7168, 256], P('pipe', 'tensor'), may hold values from -0.0625 to 0.0625
- w_out: bfloat16 [8, 7168, 256], P('pipe', 'tensor'), may hold values from -0.0625 to 0.0625
- first_moment: float32 [8, 4, 7168, 256], P('pipe', None, 'tensor'), may hold values from -6 to 6
- second_moment: float32 [8, 4, 2], P('pipe'), may hold values from 0.01 to 1
Outputs:
- grads_in: bfloat16 [8, 2, 7168, 64], P('pipe', None, 'tensor')
- update: bfloat16 [8, 4, 7168, 256], P('pipe', None, 'tensor')
- second_new: float32 [8, 4, 2], P('pipe')
The draws below stay inside these ranges and needn't reach their ends.
Inputs may be any that keep to these rules, and one draw needn't show every extreme that they name: `documents`: ids never fall along a row; each document holds 1 to 32 tokens, one exactly 32.
All inputs are finite; a program needn't handle non-finite values.
Results may differ from the reference program's by a relative error of at most 0.0308.
Values may be sent and summed in bfloat16 or wider, within the bound.
A program may use at most 128 MiB of HBM per device.

```python
import math
import jax
import jax.numpy as jnp
import numpy as np
from jax import lax

D = 7168
HEAD_DIM = 128
HEADS = 2
HD = 256
S = 64
N_PIPE = 8


def feature_rise():
    return jnp.arange(D, dtype=jnp.float32) / (D - 1)


def draw_gain(key, part):
    rise = feature_rise()
    factor = jax.random.uniform(key, (N_PIPE, D), jnp.float32, 0.8, 1.2)
    return factor * (0.5 + 1.1 * rise)[None, :]


def draw_cotangent(key, part):
    rise = feature_rise()
    noise = jnp.clip(jax.random.normal(key, (2, D, S), jnp.float32), -4.0, 4.0)
    return (noise * (0.55 + 1.1 * rise)[None, :, None]).astype(jnp.bfloat16)


def query_base(key):
    return jax.random.normal(jax.random.fold_in(key, 11), (N_PIPE, D, HD), jnp.float32) * D ** (-0.5)


def draw_w_query(key, part):
    base = query_base(key)
    return base.astype(jnp.bfloat16)


def draw_w_key(key, part):
    noise = jax.random.normal(jax.random.fold_in(key, 12), (N_PIPE, D, HD), jnp.float32) * D ** (-0.5)
    return noise.astype(jnp.bfloat16)


def block_scale(key, dims, cuts, low, high):
    level, own = 1.0, jax.random.fold_in(key, 6)
    for axis_at, parts in cuts:
        heights = jnp.exp(jax.random.uniform(jax.random.fold_in(own, axis_at), (parts,), jnp.float32, low / len(cuts), high / len(cuts)))
        level = level * jnp.repeat(heights, dims[axis_at] // parts).reshape([-1 if axis == axis_at else 1 for axis in range(len(dims))])
    return level


def profile(number_of, total, limit, slope):
    portions = [(1 << 20) // math.isqrt(grade ** slope) + 1 for grade in range(2, number_of + 1)]
    spare, holding = total - limit - (number_of - 1), [1] * (number_of - 1)
    while spare > 0:
        candidates = [i for i in range(number_of - 1) if holding[i] < limit]
        whole, left = sum([portions[i] for i in candidates]), spare
        for i in candidates:
            extra = min(limit - holding[i], max(1, left * portions[i] // whole), spare)
            holding[i] = holding[i] + extra
            spare = spare - extra
    return np.array([limit] + holding)


def uneven(stream_key, count, total, limit, lean):
    if count == 2:
        one = jax.random.randint(stream_key, (), max(1, total - limit), min(limit, total - 1) + 1)
        return jnp.stack([one, total - one])
    sizes = jnp.asarray(profile(count, total, limit, lean), jnp.int32)
    twos = (count - 1) // 2
    donor, receiver = sizes[1:1 + 2 * twos:2], sizes[2:2 + 2 * twos:2]
    slack = jnp.minimum(donor - 1, limit - receiver)
    moved = jax.random.randint(jax.random.fold_in(stream_key, 1), (twos,), 0, 1 << 20) % (slack + 1)
    sizes = sizes.at[1:1 + 2 * twos:2].set(donor - moved).at[2:2 + 2 * twos:2].set(receiver + moved)
    return sizes[jax.random.permutation(jax.random.fold_in(stream_key, 2), count)]


def normal_values(own_key, dims, scale, most, cuts=(), kind=jnp.bfloat16):
    loudness = block_scale(own_key, dims, cuts, -0.22, 0.18) if cuts else 1.0
    values = jax.random.normal(own_key, dims, jnp.float32) * scale * loudness
    return jnp.minimum(jnp.maximum(values, -most), most).astype(kind)


def setup_inputs(seed: int = 0) -> dict:
    key_list = jax.random.split(jax.random.key(seed), 11)
    return {
        "section_inputs": normal_values(key_list[0], (N_PIPE, 2, D, S), 1.0, 6.0, ((0, 8), (2, 4))),
        "cotangent": draw_cotangent(jax.random.fold_in(key_list[10], 71), 0),
        "documents": jax.vmap(lambda own: jnp.searchsorted(jnp.cumsum(uneven(own, 4, S, S // 2, 2)), jnp.arange(S), side="right"))(jax.random.split(key_list[2], 2)).reshape((2, S)).astype(jnp.int32),
        "gain": draw_gain(jax.random.fold_in(key_list[10], 71), 0),
        "w_query": draw_w_query(jax.random.fold_in(key_list[10], 71), 0),
        "w_key": draw_w_key(jax.random.fold_in(key_list[10], 71), 0),
        "w_value": normal_values(key_list[6], (N_PIPE, D, HD), D ** -0.5, 0.0625, ((0, 8), (1, 4))),
        "w_out": normal_values(key_list[7], (N_PIPE, D, HD), D ** -0.5, 0.0625, ((0, 8), (1, 4))),
        "first_moment": normal_values(key_list[8], (N_PIPE, 4, D, HD), 1.0, 6.0, ((0, 8), (2, 4)), jnp.float32),
        "second_moment": jnp.clip(jnp.exp(math.log(1.0) - 4.6051702 * jax.random.uniform(key_list[9], (N_PIPE, 4, HEADS), jnp.float32) ** block_scale(key_list[9], (N_PIPE, 4, HEADS), ((0, 8),), -0.2, 0.2)), 0.01, 1.0),
    }


EPS = 1e-06
NEG = -1e+30
BETA_ONE = 0.9
BETA_TWO = 0.95
CORRECT_ONE = 1.0 - 0.9 ** 10
CORRECT_TWO = 1.0 - 0.95 ** 10
ADAM_EPS = 1e-08

def split_heads(values):
    return values.astype(jnp.float32).reshape(values.shape[0], values.shape[1] // HEAD_DIM, HEAD_DIM)

def attend(query, keys, values, doc):
    scale = HEAD_DIM ** (-0.5)
    scores = jnp.einsum('shc,thc->hst', split_heads(query), split_heads(keys)) * scale
    positions = jnp.arange(query.shape[0], dtype=jnp.int32)
    allowed = (doc[:, None] == doc[None, :]) & (positions[None, :] <= positions[:, None])
    scores = jnp.where(allowed[None], scores, NEG)
    top = lax.optimization_barrier(jnp.max(scores, axis=2, keepdims=True))
    expo = jnp.exp(scores - top)
    probs = expo / lax.optimization_barrier(jnp.sum(expo, axis=2, keepdims=True))
    probs_b = probs.astype(jnp.bfloat16)
    mixed = jnp.einsum('hst,thc->shc', probs_b.astype(jnp.float32), split_heads(values))
    return (probs, probs_b, mixed.astype(jnp.bfloat16).reshape(query.shape))

def section_backward(inputs, upstream, gain, w_query, w_key, w_value, w_out, doc):
    widef = inputs.astype(jnp.float32)
    scaled = (widef * gain[:, None]).astype(jnp.bfloat16)
    inverse = lax.rsqrt(lax.optimization_barrier(jnp.mean(widef * widef, axis=0)) + EPS)
    raws = [jnp.dot(scaled.T, weight, preferred_element_type=jnp.float32) for weight in (w_query, w_key, w_value)]
    query, keys, values = [(raw * inverse[:, None]).astype(jnp.bfloat16) for raw in raws]
    probs, probs_b, mixed = attend(query, keys, values, doc)
    dmixed = jnp.dot(upstream.T, w_out, preferred_element_type=jnp.float32).astype(jnp.bfloat16)
    grad_out = jnp.dot(upstream, mixed, preferred_element_type=jnp.float32)
    scale = HEAD_DIM ** (-0.5)
    dprobs = jnp.einsum('shc,thc->hst', split_heads(dmixed), split_heads(values))
    delta = jnp.einsum('shc,shc->hs', split_heads(dmixed), split_heads(mixed))
    dscores = (probs * (dprobs - delta[:, :, None]) * scale).astype(jnp.bfloat16).astype(jnp.float32)
    seq = query.shape[0]
    dquery = jnp.einsum('hst,thc->shc', dscores, split_heads(keys)).reshape(seq, -1)
    dkeys = jnp.einsum('hst,shc->thc', dscores, split_heads(query)).reshape(seq, -1)
    dvalues = jnp.einsum('hst,shc->thc', probs_b.astype(jnp.float32), split_heads(dmixed)).reshape(seq, -1)
    cotans = (dquery, dkeys, dvalues)
    stat = sum((lax.optimization_barrier(jnp.sum(grad * raw, axis=1)) for grad, raw in zip(cotans, raws)))
    scaled_grads = [(grad * inverse[:, None]).astype(jnp.bfloat16) for grad in cotans]
    grads = [jnp.dot(scaled, grad, preferred_element_type=jnp.float32) for grad in scaled_grads]
    dscaled = sum((jnp.dot(weight, grad.T, preferred_element_type=jnp.float32) for weight, grad in zip((w_query, w_key, w_value), scaled_grads)))
    result = upstream.astype(jnp.float32) + gain[:, None] * dscaled - widef * (inverse ** 3 * stat / D)[None, :]
    return (result.astype(jnp.bfloat16), jnp.stack(grads + [grad_out]))

def reference(section_inputs, cotangent, documents, gain, w_query, w_key, w_value, w_out, first_moment, second_moment):
    sections = section_inputs.shape[0]
    grads_in = [[None, None] for unused in range(sections)]
    weight_grads = [None] * sections
    for which in range(2):
        upstream = cotangent[which]
        order = range(sections - 1, -1, -1) if which == 0 else range(sections)
        for section in order:
            result, grads = section_backward(section_inputs[section, which], upstream, gain[section], w_query[section], w_key[section], w_value[section], w_out[section], documents[which])
            grads_in[section][which] = result
            weight_grads[section] = grads if weight_grads[section] is None else weight_grads[section] + grads
            upstream = result
    updates = []
    seconds = []
    heads = w_query.shape[2] // HEAD_DIM
    for section in range(sections):
        grads = weight_grads[section]
        per_head = lax.optimization_barrier(jnp.sum((grads * grads).reshape(4, grads.shape[1], heads, HEAD_DIM), axis=(1, 3)))
        second = BETA_TWO * second_moment[section] + (1.0 - BETA_TWO) * per_head / (D * HEAD_DIM)
        moment = BETA_ONE * first_moment[section] + (1.0 - BETA_ONE) * grads
        denom = jnp.sqrt(second / CORRECT_TWO) + ADAM_EPS
        step = (moment / CORRECT_ONE).reshape(4, grads.shape[1], heads, HEAD_DIM) / denom[:, None, :, None]
        updates.append(step.reshape(grads.shape).astype(jnp.bfloat16))
        seconds.append(second)
    grads_all = jnp.stack([jnp.stack(pair) for pair in grads_in])
    return (grads_all, jnp.stack(updates), jnp.stack(seconds))
```

```python
import functools

import jax
import jax.numpy as jnp
from jax import lax
from jax.experimental import pallas as pl
from jax.experimental.pallas import tpu as pltpu
from jax.sharding import PartitionSpec as P

HEAD_DIM = 128
EPS = 1e-06
NEG = -1e30
BETA_ONE = 0.9
BETA_TWO = 0.95
CORRECT_ONE = 1.0 - 0.9**10
CORRECT_TWO = 1.0 - 0.95**10
ADAM_EPS = 1e-08
MESH = pl.DeviceIdType.MESH
F32 = jnp.float32
BF16 = jnp.bfloat16


def dot(a, b, contract=(1, 0)):
    return lax.dot_general(
        a, b, (((contract[0],), (contract[1],)), ((), ())), preferred_element_type=F32
    )


def relay_kernel(
    n_pipe,
    n_tensor,
    x_hbm,
    cot_hbm,
    doc_ref,
    gain_hbm,
    wq_hbm,
    wk_hbm,
    wv_hbm,
    wo_hbm,
    first_hbm,
    second_ref,
    grads_ref,
    moment_ref,
    second_out_ref,
    scale_ref,
    x_ref,
    gain_ref,
    w_buf,
    u_buf,
    wn_buf,
    raw_send,
    raw_recv,
    qkv_buf,
    dm_start,
    dm_send,
    dm_recv,
    cross,
    cross_x,
    ahead,
    right_s,
    probs_s,
    inv_s,
    coeff_s,
    scaled_buf,
    left_s,
    gram_s,
    tot_send,
    tot_recv,
    rs_ss,
    rs_rs,
    ag_ss,
    ag_rs,
    start_ss,
    dm_ss,
    dm_rs,
    u_ss,
    u_rs,
    wn_ss,
    wn_rs,
    tot_ss,
    tot_rs,
    load_sem,
    cot_sem,
    moment_sem,
):
    me = lax.axis_index("pipe")
    rank = lax.axis_index("tensor")
    last = n_pipe - 1
    _, seq, width = x_ref.shape
    cols = wq_hbm.shape[1]
    heads = cols // HEAD_DIM
    full = width * n_tensor
    scale = HEAD_DIM ** (-0.5)
    w_refs = tuple(w_buf.at[i] for i in range(3))
    wo_ref = w_buf.at[3]
    sources = (x_hbm, gain_hbm, wq_hbm, wk_hbm, wv_hbm, wo_hbm)
    targets = (x_ref, gain_ref) + tuple(w_buf.at[i] for i in range(4))
    loads = [
        pltpu.make_async_copy(source, target, load_sem.at[i])
        for i, (source, target) in enumerate(zip(sources, targets))
    ]
    load_moment = pltpu.make_async_copy(first_hbm, moment_ref, moment_sem)
    peers = [lax.rem(rank + step, n_tensor) for step in range(1, n_tensor)]
    lower = 2 * me < n_pipe
    first = jnp.where(lower, 1, 0).astype(jnp.int32)
    near = 1 - lax.rem(me, 2)
    outer = (me == 0) | (me == last)
    early = outer | (me == 1) | (me == last - 1)
    shares = min(n_tensor, seq // 16)
    stride = n_tensor // shares
    chunk = seq // shares
    pieces = 2 if width % 256 == 0 else 1
    piece = width // pieces

    def load_cot(j):
        return pltpu.make_async_copy(cot_hbm.at[j], u_buf.at[j], cot_sem)

    def rs_copy(j, owner, slot):
        return pltpu.make_async_remote_copy(
            src_ref=raw_send.at[j, pl.ds(owner * chunk, chunk)],
            dst_ref=raw_recv.at[j, slot],
            send_sem=rs_ss.at[j, owner],
            recv_sem=rs_rs.at[j, slot],
            device_id=(me, owner * stride),
            device_id_type=MESH,
        )

    def ag_copy(j, owner, peer):
        rows = pl.ds(pl.multiple_of(owner * chunk, chunk), chunk)
        return pltpu.make_async_remote_copy(
            src_ref=qkv_buf.at[j, rows],
            dst_ref=qkv_buf.at[j, rows],
            send_sem=ag_ss.at[j, peer],
            recv_sem=ag_rs.at[j, owner],
            device_id=(me, peer),
            device_id_type=MESH,
        )

    def start_copy(j, peer, slot):
        return pltpu.make_async_remote_copy(
            src_ref=dm_start,
            dst_ref=dm_recv.at[j, slot],
            send_sem=start_ss.at[peer],
            recv_sem=dm_rs.at[j, slot],
            device_id=(me, peer),
            device_id_type=MESH,
        )

    def dm_copy(j, nxt, peer, slot):
        return pltpu.make_async_remote_copy(
            src_ref=dm_send.at[j],
            dst_ref=dm_recv.at[j, slot],
            send_sem=dm_ss.at[j, peer],
            recv_sem=dm_rs.at[j, slot],
            device_id=(nxt, peer),
            device_id_type=MESH,
        )

    def u_copy(j, nxt, c):
        part = pl.ds(c * piece, piece)
        return pltpu.make_async_remote_copy(
            src_ref=grads_ref.at[j, :, part],
            dst_ref=u_buf.at[j, :, part],
            send_sem=u_ss.at[j, c],
            recv_sem=u_rs.at[j, c],
            device_id=(nxt, rank),
            device_id_type=MESH,
        )

    def wn_copy(j, target, c):
        part = pl.ds(c * piece, piece)
        return pltpu.make_async_remote_copy(
            src_ref=wo_hbm.at[part],
            dst_ref=wn_buf.at[j, part],
            send_sem=wn_ss.at[j, c],
            recv_sem=wn_rs.at[j, c],
            device_id=(target, rank),
            device_id_type=MESH,
        )

    def tot_copy(peer, slot):
        return pltpu.make_async_remote_copy(
            src_ref=tot_send,
            dst_ref=tot_recv.at[slot],
            send_sem=tot_ss.at[peer],
            recv_sem=tot_rs.at[slot],
            device_id=(me, peer),
            device_id_type=MESH,
        )

    barrier = pltpu.get_barrier_semaphore()
    for peer in peers:
        pl.semaphore_signal(barrier, inc=1, device_id=(me, peer), device_id_type=MESH)

    @pl.when(me > 0)
    def _():
        for t in range(n_tensor):
            pl.semaphore_signal(barrier, inc=1, device_id=(me - 1, t), device_id_type=MESH)

    @pl.when(me < last)
    def _():
        for t in range(n_tensor):
            pl.semaphore_signal(barrier, inc=1, device_id=(me + 1, t), device_id_type=MESH)

    for load in loads:
        load.start()
    for j, start in ((0, last), (1, 0)):

        @pl.when(me == start)
        def _(j=j):
            load_cot(j).start()

    loads[0].wait()
    loads[1].wait()
    gain_row = gain_ref[...]
    for j in range(2):
        wide = x_ref[j].astype(F32)
        scaled_buf[j * seq : (j + 1) * seq, :] = (wide * gain_row).astype(BF16)
        squares = jnp.sum(wide * wide, axis=1, keepdims=True)
        high = squares.astype(BF16).astype(F32)
        lane = lax.broadcasted_iota(jnp.int32, (seq, HEAD_DIM), 1)
        raw_send[j, :, 3 * cols :] = jnp.where(lane == 0, high, squares - high).astype(BF16)
    sides = jnp.where(outer, 1, 2).astype(jnp.int32)
    pl.semaphore_wait(barrier, n_tensor - 1 + n_tensor * sides)

    def send_weights(j):
        target = me + 1 - 2 * j

        @pl.when((target >= 0) & (target <= last))
        def _():
            for c in range(pieces):
                wn_copy(j, target, c).start()

    send_weights(1 - near)
    send_weights(near)
    for i, w_ref in enumerate(w_refs):
        loads[2 + i].wait()
        part = dot(scaled_buf[...], w_ref[...]).astype(BF16)
        raw_send[0, :, i * cols : (i + 1) * cols] = part[:seq]
        raw_send[1, :, i * cols : (i + 1) * cols] = part[seq:]

    def scatter(j):
        for owner in range(shares):

            @pl.when(rank != owner * stride)
            def _(owner=owner):
                rs_copy(j, owner, rank).start()

    scatter(first)
    loads[5].wait()
    for j, start in ((0, last), (1, 0)):

        @pl.when(me == start)
        def _(j=j):
            load_cot(j).wait()
            dm_start[...] = dot(u_buf[j], wo_ref[...]).astype(BF16)
            dm_recv[j, rank] = dm_start[...]
            for peer in peers:
                start_copy(j, peer, rank).start()

    load_moment.start()

    def crossing(j):
        for c in range(pieces):
            wn_copy(j, me, c).wait_recv()
        turned = (wn_buf[j].T.astype(F32) * gain_ref[...]).astype(BF16)
        for i, w_ref in enumerate(w_refs):
            part = dot(turned, w_ref[...]).astype(BF16)
            cross[j, i * cols : (i + 1) * cols, :] = part.T
        cross_x[j] = dot(x_ref[j], wn_buf[j])

    @pl.when(me != near * last)
    def _():
        crossing(near)

    def forward(j):
        @pl.when(lax.rem(rank, stride) == 0)
        def _():
            owner = lax.div(rank, stride)
            rows = pl.ds(pl.multiple_of(owner * chunk, chunk), chunk)
            total = raw_send[j, rows].astype(F32)
            for peer in peers:
                rs_copy(j, 0, peer).wait_recv()
            for peer in peers:
                total = total + raw_recv[j, peer].astype(F32)
            squares = total[:, 3 * cols : 3 * cols + 1] + total[:, 3 * cols + 1 : 3 * cols + 2]
            inverse = lax.rsqrt(squares / full + EPS)
            high = inverse.astype(BF16).astype(F32)
            lane = lax.broadcasted_iota(jnp.int32, (chunk, HEAD_DIM), 1)
            qkv_buf[j, rows, : 3 * cols] = (total[:, : 3 * cols] * inverse).astype(BF16)
            qkv_buf[j, rows, 3 * cols :] = jnp.where(lane == 0, high, inverse - high).astype(BF16)
            for peer in peers:
                ag_copy(j, owner, peer).start()

        @pl.when(j == first)
        def _():
            scatter(1 - first)

        for owner in range(shares):

            @pl.when(rank != owner * stride)
            def _(owner=owner):
                ag_copy(j, owner, rank).wait_recv()

        coded = qkv_buf[j, :, 3 * cols :].astype(F32)
        inverse = coded[:, 0:1] + coded[:, 1:2]
        inv_s[j] = jnp.broadcast_to(inverse, (seq, HEAD_DIM))
        qkv = qkv_buf[j, :, : 3 * cols]
        row = lax.broadcasted_iota(jnp.int32, (seq, seq), 0)
        col = lax.broadcasted_iota(jnp.int32, (seq, seq), 1)
        doc = jnp.broadcast_to(doc_ref[j].astype(F32), (seq, seq))
        allowed = (doc.T == doc) & (col <= row)
        for h in range(heads):
            lo, hi = h * HEAD_DIM, (h + 1) * HEAD_DIM
            query, keys = qkv[:, lo:hi], qkv[:, cols + lo : cols + hi]
            values = qkv[:, 2 * cols + lo : 2 * cols + hi]
            scores = jnp.where(allowed, dot(query, keys, (1, 1)) * scale, NEG)
            expo = jnp.exp(scores - jnp.max(scores, axis=1, keepdims=True))
            probs = expo / jnp.sum(expo, axis=1, keepdims=True)
            probs_s[j, h] = probs
            right_s[j, :, 3 * cols + lo : 3 * cols + hi] = dot(probs.astype(BF16), values).astype(BF16)

        @pl.when(j != first)
        def _():
            left_s[0] = scaled_buf[...].T
            gram_s[...] = dot(scaled_buf[...], scaled_buf[...], (1, 1))

    def event(j):
        at_end = me == j * last
        at_start = me == (1 - j) * last
        going = jnp.logical_not(at_end)
        nxt = me + 2 * j - 1

        @pl.when(going & (j != near))
        def _():
            crossing(j)

        def arrive(c):
            @pl.when(jnp.logical_not(at_start))
            def _():
                u_copy(j, me, c).wait_recv()

            @pl.when(going)
            def _():
                part = slice(c * piece, (c + 1) * piece)
                term = dot(u_buf[j, :, part], wn_buf[j, part])
                ahead[...] = term if c == 0 else ahead[...] + term

        for c in range(pieces - 1):
            arrive(c)
        for slot in range(n_tensor):

            @pl.when(jnp.logical_not(at_start & (rank == slot)))
            def _(slot=slot):
                dm_copy(j, me, slot, slot).wait_recv()

        total = dm_recv[j, 0].astype(F32)
        for slot in range(1, n_tensor):
            total = total + dm_recv[j, slot].astype(F32)
        dmixed = total.astype(BF16)
        inverse = inv_s[j][:, :1]
        stat = jnp.zeros((seq, 1), F32)
        for h in range(heads):
            lo, hi = h * HEAD_DIM, (h + 1) * HEAD_DIM
            query, keys = qkv_buf[j, :, lo:hi], qkv_buf[j, :, cols + lo : cols + hi]
            values = qkv_buf[j, :, 2 * cols + lo : 2 * cols + hi]
            mixed = right_s[j, :, 3 * cols + lo : 3 * cols + hi]
            probs = probs_s[j, h]
            upper = dmixed[:, lo:hi]
            dprobs = dot(upper, values, (1, 1))
            delta = jnp.sum(upper.astype(F32) * mixed.astype(F32), axis=1, keepdims=True)
            dscores = (probs * (dprobs - delta) * scale).astype(BF16)
            grads = (
                dot(dscores, keys),
                dot(dscores, query, (0, 0)),
                dot(probs.astype(BF16), upper, (0, 0)),
            )
            for i, (grad, saved) in enumerate(zip(grads, (query, keys, values))):
                at = i * cols
                stat = stat + jnp.sum(grad * saved.astype(F32), axis=1, keepdims=True)
                right_s[j, :, at + lo : at + hi] = (grad * inverse).astype(BF16)
        coeff = inverse * inverse * stat / full
        coeff_s[j] = jnp.broadcast_to(coeff, (seq, HEAD_DIM))
        arrive(pieces - 1)

        @pl.when(going)
        def _():
            right = right_s[j, :, : 3 * cols]
            step = ahead[...] + dot(right, cross[j]) - coeff * cross_x[j]
            dm_send[j] = step.astype(BF16)
            for peer in range(n_tensor):
                dm_copy(j, nxt, peer, rank).start()
            for c in range(pieces):
                finish(j, c)
                u_copy(j, nxt, c).start()

    def finish(j, c):
        part = slice(c * piece, (c + 1) * piece)
        coeff = coeff_s[j][:, :1]
        dscaled = None
        for i in range(3):
            term = dot(right_s[j, :, i * cols : (i + 1) * cols], w_buf[i, part], (1, 1))
            dscaled = term if dscaled is None else dscaled + term
        result = (
            u_buf[j, :, part].astype(F32)
            + gain_ref[:, part] * dscaled
            - x_ref[j, :, part].astype(F32) * coeff
        )
        grads_ref[j, :, part] = result.astype(BF16)

    def turn(k, unused):
        swap = jnp.where(early, 1, 0).astype(jnp.int32)
        second_half = k // 2
        other = lax.rem(k, 2)
        which = jnp.where(swap == 1, second_half, other)
        is_event = jnp.where(swap == 1, other, second_half)
        j = lax.rem(first + which, 2)

        @pl.when(is_event == 0)
        def _():
            forward(j)

        @pl.when(is_event == 1)
        def _():
            event(j)

        return unused

    lax.fori_loop(0, 4, turn, 0)

    stacked = jnp.concatenate([u_buf[0], u_buf[1]], axis=0)
    for m in range(4):
        gram = gram_s[...] if m < 3 else dot(stacked, stacked, (1, 1))
        for h in range(heads):
            lo = m * cols + h * HEAD_DIM
            both = jnp.concatenate(
                [right_s[0, :, lo : lo + HEAD_DIM], right_s[1, :, lo : lo + HEAD_DIM]], axis=0
            )
            sums = jnp.sum(gram * dot(both, both, (1, 1)), axis=0, keepdims=True)
            tot_send[m * heads + h : m * heads + h + 1, :] = sums
    tot_recv[rank] = tot_send[...]
    for peer in peers:
        tot_copy(peer, rank).start()

    @pl.when(outer)
    def _():
        for c in range(pieces):
            finish(1 - first, c)

    left_s[1] = stacked.T
    load_moment.wait()
    for m in range(4):
        both = jnp.concatenate(
            [right_s[0, :, m * cols : (m + 1) * cols], right_s[1, :, m * cols : (m + 1) * cols]], axis=0
        )
        for c in range(pieces):
            part = slice(c * piece, (c + 1) * piece)
            grads = dot(left_s[m // 3, part], both)
            moment_ref[m, part] = BETA_ONE * moment_ref[m, part] + (1.0 - BETA_ONE) * grads
    for peer in peers:
        tot_copy(peer, peer).wait_recv()
    total = tot_recv[0]
    for slot in range(1, n_tensor):
        total = total + tot_recv[slot]
    totals = jnp.sum(total, axis=1, keepdims=True)
    for m in range(4):
        for h in range(heads):
            at = m * heads + h
            second = BETA_TWO * second_ref[h : h + 1, m : m + 1] + (1.0 - BETA_TWO) * totals[
                at : at + 1
            ] / (full * HEAD_DIM)
            second_out_ref[h : h + 1, m : m + 1] = second
            denom = jnp.sqrt(second / CORRECT_TWO) + ADAM_EPS
            scale_ref[at : at + 1, :] = jnp.broadcast_to(1.0 / (denom * CORRECT_ONE), (1, HEAD_DIM))

    for j in range(2):
        for owner in range(shares):

            @pl.when(rank != owner * stride)
            def _(j=j, owner=owner):
                rs_copy(j, owner, rank).wait_send()

        @pl.when(lax.rem(rank, stride) == 0)
        def _(j=j):
            for peer in peers:
                ag_copy(j, lax.div(rank, stride), peer).wait_send()

    for peer in peers:
        tot_copy(peer, rank).wait_send()
    for j, start in ((0, last), (1, 0)):

        @pl.when(me == start)
        def _(j=j):
            for peer in peers:
                start_copy(j, peer, rank).wait_send()

        @pl.when(me != j * last)
        def _(j=j):
            nxt = me + 2 * j - 1
            for peer in range(n_tensor):
                dm_copy(j, nxt, peer, rank).wait_send()
            for c in range(pieces):
                u_copy(j, nxt, c).wait_send()

        @pl.when(me != (1 - j) * last)
        def _(j=j):
            for c in range(pieces):
                wn_copy(j, me + 1 - 2 * j, c).wait_send()


def update_kernel(
    moment_ref, scale_ref, grads_ref, second_ref, out_hbm, grads_hbm, second_out_ref, out_buf, out_sem, grads_sem
):
    count, width, cols = moment_ref.shape
    heads = cols // HEAD_DIM
    pieces = 2 if width % 256 == 0 else 1
    piece = width // pieces
    copy_grads = pltpu.make_async_copy(grads_ref, grads_hbm, grads_sem)
    copy_grads.start()
    copies = []
    for m in range(count):
        row = jnp.concatenate([scale_ref[m * heads + h : m * heads + h + 1] for h in range(heads)], axis=1)
        for c in range(pieces):
            part = pl.ds(c * piece, piece)
            out_buf[m, part] = (moment_ref[m, part] * row).astype(BF16)
            copy = pltpu.make_async_copy(out_buf.at[m, part], out_hbm.at[m, part], out_sem.at[m, c])
            copy.start()
            copies.append(copy)
    second_out_ref[...] = second_ref[...]
    for copy in copies:
        copy.wait()
    copy_grads.wait()


def on_device(
    n_pipe,
    n_tensor,
    section_inputs,
    cotangent,
    documents,
    gain,
    w_query,
    w_key,
    w_value,
    w_out,
    first_moment,
    second_moment,
):
    x = jnp.swapaxes(section_inputs[0], 1, 2)
    cot = jnp.swapaxes(cotangent, 1, 2)
    _, seq, width = x.shape
    cols = w_query.shape[2]
    heads = cols // HEAD_DIM
    rows = 4 * heads
    raw_cols = 3 * cols + HEAD_DIM
    shares = min(n_tensor, seq // 16)
    pieces = 2 if width % 256 == 0 else 1
    vmem = pl.BlockSpec(memory_space=pltpu.VMEM)
    hbm = pl.BlockSpec(memory_space=pltpu.HBM)
    dma = pltpu.SemaphoreType.DMA
    held = functools.partial(pltpu.with_memory_space_constraint, memory_space=pltpu.HBM)
    grads, moment, second, scales = pl.pallas_call(
        functools.partial(relay_kernel, n_pipe, n_tensor),
        name="relay",
        out_shape=(
            pltpu.VMEM((2, seq, width), BF16),
            pltpu.VMEM((4, width, cols), F32),
            pltpu.VMEM((heads, 4), F32),
            pltpu.VMEM((rows, HEAD_DIM), F32),
        ),
        in_specs=[hbm, hbm, vmem] + [hbm] * 6 + [vmem],
        out_specs=(vmem,) * 4,
        scratch_shapes=[
            pltpu.VMEM((2, seq, width), BF16),
            pltpu.VMEM((1, width), F32),
            pltpu.VMEM((4, width, cols), BF16),
            pltpu.VMEM((2, seq, width), BF16),
            pltpu.VMEM((2, width, cols), BF16),
            pltpu.VMEM((2, seq, raw_cols), BF16),
            pltpu.VMEM((2, n_tensor, seq // shares, raw_cols), BF16),
            pltpu.VMEM((2, seq, raw_cols), BF16),
            pltpu.VMEM((seq, cols), BF16),
            pltpu.VMEM((2, seq, cols), BF16),
            pltpu.VMEM((2, n_tensor, seq, cols), BF16),
            pltpu.VMEM((2, 3 * cols, cols), BF16),
            pltpu.VMEM((2, seq, cols), F32),
            pltpu.VMEM((seq, cols), F32),
            pltpu.VMEM((2, seq, 4 * cols), BF16),
            pltpu.VMEM((2, heads, seq, seq), F32),
            pltpu.VMEM((2, seq, HEAD_DIM), F32),
            pltpu.VMEM((2, seq, HEAD_DIM), F32),
            pltpu.VMEM((2 * seq, width), BF16),
            pltpu.VMEM((2, width, 2 * seq), BF16),
            pltpu.VMEM((2 * seq, 2 * seq), F32),
            pltpu.VMEM((rows, 2 * seq), F32),
            pltpu.VMEM((n_tensor, rows, 2 * seq), F32),
            dma((2, shares)),
            dma((2, n_tensor)),
            dma((2, n_tensor)),
            dma((2, shares)),
            dma((n_tensor,)),
            dma((2, n_tensor)),
            dma((2, n_tensor)),
            dma((2, pieces)),
            dma((2, pieces)),
            dma((2, pieces)),
            dma((2, pieces)),
            dma((n_tensor,)),
            dma((n_tensor,)),
            dma((6,)),
            dma,
            dma,
        ],
        compiler_params=pltpu.CompilerParams(
            collective_id=0, has_side_effects=True, vmem_limit_bytes=48 * 2**20
        ),
    )(
        held(x),
        held(cot),
        documents[:, None, :],
        held(gain),
        held(w_query[0]),
        held(w_key[0]),
        held(w_value[0]),
        held(w_out[0]),
        held(first_moment[0]),
        jnp.swapaxes(second_moment[0], 0, 1),
    )
    update, grads, second = pl.pallas_call(
        update_kernel,
        name="update",
        out_shape=(
            jax.ShapeDtypeStruct((4, width, cols), BF16),
            jax.ShapeDtypeStruct((2, seq, width), BF16),
            jax.ShapeDtypeStruct((heads, 4), F32),
        ),
        in_specs=[vmem] * 4,
        out_specs=(hbm, hbm, vmem),
        scratch_shapes=[
            pltpu.VMEM((4, width, cols), BF16),
            dma((4, pieces)),
            dma,
        ],
        compiler_params=pltpu.CompilerParams(vmem_limit_bytes=32 * 2**20),
    )(moment, scales, grads, second)
    return (
        jnp.swapaxes(grads, 1, 2)[None],
        update[None],
        jnp.swapaxes(second, 0, 1)[None],
    )


def solution(mesh):
    placed = (
        P("pipe", None, "tensor", None),
        P(None, "tensor", None),
        P(),
        P("pipe", "tensor"),
        P("pipe", "tensor", None),
        P("pipe", "tensor", None),
        P("pipe", "tensor", None),
        P("pipe", "tensor", None),
        P("pipe", None, "tensor", None),
        P("pipe", None, None),
    )
    return jax.shard_map(
        functools.partial(on_device, mesh.shape["pipe"], mesh.shape["tensor"]),
        mesh=mesh,
        in_specs=placed,
        out_specs=(
            P("pipe", None, "tensor", None),
            P("pipe", None, "tensor", None),
            P("pipe", None, None),
        ),
        check_vma=False,
    )
```

```python
import functools

import jax
import jax.numpy as jnp
from jax import lax
from jax.experimental import pallas as pl
from jax.experimental.pallas import tpu as pltpu
from jax.sharding import PartitionSpec as P

HEAD_DIM = 128
EPS = 1e-06
NEG = -1e30
BETA_ONE = 0.9
BETA_TWO = 0.95
CORRECT_ONE = 1.0 - 0.9**10
CORRECT_TWO = 1.0 - 0.95**10
ADAM_EPS = 1e-08
MESH = pl.DeviceIdType.MESH
F32 = jnp.float32
BF16 = jnp.bfloat16


def dot(a, b, contract=(1, 0)):
    return lax.dot_general(
        a, b, (((contract[0],), (contract[1],)), ((), ())), preferred_element_type=F32
    )


def relay_kernel(
    n_pipe,
    n_tensor,
    x_hbm,
    cot_hbm,
    doc_ref,
    gain_hbm,
    wq_hbm,
    wk_hbm,
    wv_hbm,
    wo_hbm,
    first_hbm,
    second_ref,
    grads_ref,
    moment_ref,
    second_out_ref,
    scale_ref,
    x_ref,
    gain_ref,
    w_buf,
    u_buf,
    wn_buf,
    raw_send,
    raw_recv,
    qkv_buf,
    dm_start,
    dm_send,
    dm_recv,
    cross,
    cross_x,
    ahead,
    right_s,
    probs_s,
    inv_s,
    coeff_s,
    scaled_buf,
    left_s,
    gram_s,
    tot_send,
    tot_recv,
    rs_ss,
    rs_rs,
    ag_ss,
    ag_rs,
    start_ss,
    dm_ss,
    dm_rs,
    u_ss,
    u_rs,
    wn_ss,
    wn_rs,
    tot_ss,
    tot_rs,
    load_sem,
    cot_sem,
    moment_sem,
):
    me = lax.axis_index("pipe")
    rank = lax.axis_index("tensor")
    last = n_pipe - 1
    _, seq, width = x_ref.shape
    cols = wq_hbm.shape[1]
    heads = cols // HEAD_DIM
    full = width * n_tensor
    scale = HEAD_DIM ** (-0.5)
    w_refs = tuple(w_buf.at[i] for i in range(3))
    wo_ref = w_buf.at[3]
    sources = (x_hbm, gain_hbm, wq_hbm, wk_hbm, wv_hbm, wo_hbm)
    targets = (x_ref, gain_ref) + tuple(w_buf.at[i] for i in range(4))
    loads = [
        pltpu.make_async_copy(source, target, load_sem.at[i])
        for i, (source, target) in enumerate(zip(sources, targets))
    ]
    load_moment = pltpu.make_async_copy(first_hbm, moment_ref, moment_sem)
    peers = [lax.rem(rank + step, n_tensor) for step in range(1, n_tensor)]
    lower = 2 * me < n_pipe
    first = jnp.where(lower, 1, 0).astype(jnp.int32)
    near = 1 - lax.rem(me, 2)
    outer = (me == 0) | (me == last)
    early = outer | (me == 1) | (me == last - 1)
    shares = min(n_tensor, seq // 16)
    stride = n_tensor // shares
    chunk = seq // shares
    pieces = 2 if width % 256 == 0 else 1
    piece = width // pieces

    def load_cot(j):
        return pltpu.make_async_copy(cot_hbm.at[j], u_buf.at[j], cot_sem)

    def rs_copy(j, owner, slot):
        return pltpu.make_async_remote_copy(
            src_ref=raw_send.at[j, pl.ds(owner * chunk, chunk)],
            dst_ref=raw_recv.at[j, slot],
            send_sem=rs_ss.at[j, owner],
            recv_sem=rs_rs.at[j, slot],
            device_id=(me, owner * stride),
            device_id_type=MESH,
        )

    def ag_copy(j, owner, peer):
        rows = pl.ds(pl.multiple_of(owner * chunk, chunk), chunk)
        return pltpu.make_async_remote_copy(
            src_ref=qkv_buf.at[j, rows],
            dst_ref=qkv_buf.at[j, rows],
            send_sem=ag_ss.at[j, peer],
            recv_sem=ag_rs.at[j, owner],
            device_id=(me, peer),
            device_id_type=MESH,
        )

    def start_copy(j, peer, slot):
        return pltpu.make_async_remote_copy(
            src_ref=dm_start,
            dst_ref=dm_recv.at[j, slot],
            send_sem=start_ss.at[peer],
            recv_sem=dm_rs.at[j, slot],
            device_id=(me, peer),
            device_id_type=MESH,
        )

    def dm_copy(j, nxt, peer, slot):
        return pltpu.make_async_remote_copy(
            src_ref=dm_send.at[j],
            dst_ref=dm_recv.at[j, slot],
            send_sem=dm_ss.at[j, peer],
            recv_sem=dm_rs.at[j, slot],
            device_id=(nxt, peer),
            device_id_type=MESH,
        )

    def u_copy(j, nxt, c):
        part = pl.ds(c * piece, piece)
        return pltpu.make_async_remote_copy(
            src_ref=grads_ref.at[j, :, part],
            dst_ref=u_buf.at[j, :, part],
            send_sem=u_ss.at[j, c],
            recv_sem=u_rs.at[j, c],
            device_id=(nxt, rank),
            device_id_type=MESH,
        )

    def wn_copy(j, target, c):
        part = pl.ds(c * piece, piece)
        return pltpu.make_async_remote_copy(
            src_ref=wo_hbm.at[part],
            dst_ref=wn_buf.at[j, part],
            send_sem=wn_ss.at[j, c],
            recv_sem=wn_rs.at[j, c],
            device_id=(target, rank),
            device_id_type=MESH,
        )

    def tot_copy(peer, slot):
        return pltpu.make_async_remote_copy(
            src_ref=tot_send,
            dst_ref=tot_recv.at[slot],
            send_sem=tot_ss.at[peer],
            recv_sem=tot_rs.at[slot],
            device_id=(me, peer),
            device_id_type=MESH,
        )

    barrier = pltpu.get_barrier_semaphore()
    for peer in peers:
        pl.semaphore_signal(barrier, inc=1, device_id=(me, peer), device_id_type=MESH)

    @pl.when(me > 0)
    def _():
        for t in range(n_tensor):
            pl.semaphore_signal(barrier, inc=1, device_id=(me - 1, t), device_id_type=MESH)

    @pl.when(me < last)
    def _():
        for t in range(n_tensor):
            pl.semaphore_signal(barrier, inc=1, device_id=(me + 1, t), device_id_type=MESH)

    for load in loads:
        load.start()
    for j, start in ((0, last), (1, 0)):

        @pl.when(me == start)
        def _(j=j):
            load_cot(j).start()

    loads[0].wait()
    loads[1].wait()
    gain_row = gain_ref[...]
    for j in range(2):
        wide = x_ref[j].astype(F32)
        scaled_buf[j * seq : (j + 1) * seq, :] = (wide * gain_row).astype(BF16)
        squares = jnp.sum(wide * wide, axis=1, keepdims=True)
        high = squares.astype(BF16).astype(F32)
        lane = lax.broadcasted_iota(jnp.int32, (seq, HEAD_DIM), 1)
        raw_send[j, :, 3 * cols :] = jnp.where(lane == 0, high, squares - high).astype(BF16)
    sides = jnp.where(outer, 1, 2).astype(jnp.int32)
    pl.semaphore_wait(barrier, n_tensor - 1 + n_tensor * sides)

    def send_weights(j, urgent):
        target = me + 1 - 2 * j
        hurry = (j != near) | (target == 1) | (target == last - 1)

        @pl.when((target >= 0) & (target <= last) & (hurry == urgent))
        def _():
            for c in range(pieces):
                wn_copy(j, target, c).start()

    send_weights(1 - near, True)
    send_weights(near, True)
    for i, w_ref in enumerate(w_refs):
        loads[2 + i].wait()
        part = dot(scaled_buf[...], w_ref[...]).astype(BF16)
        raw_send[0, :, i * cols : (i + 1) * cols] = part[:seq]
        raw_send[1, :, i * cols : (i + 1) * cols] = part[seq:]

    def scatter(j):
        for owner in range(shares):

            @pl.when(rank != owner * stride)
            def _(owner=owner):
                rs_copy(j, owner, rank).start()

    scatter(first)
    loads[5].wait()
    for j, start in ((0, last), (1, 0)):

        @pl.when(me == start)
        def _(j=j):
            load_cot(j).wait()
            dm_start[...] = dot(u_buf[j], wo_ref[...]).astype(BF16)
            dm_recv[j, rank] = dm_start[...]
            for peer in peers:
                start_copy(j, peer, rank).start()

    load_moment.start()

    def crossing(j):
        for c in range(pieces):
            wn_copy(j, me, c).wait_recv()
        turned = (wn_buf[j].T.astype(F32) * gain_ref[...]).astype(BF16)
        for i, w_ref in enumerate(w_refs):
            part = dot(turned, w_ref[...]).astype(BF16)
            cross[j, i * cols : (i + 1) * cols, :] = part.T
        cross_x[j] = dot(x_ref[j], wn_buf[j])

    @pl.when(me != near * last)
    def _():
        crossing(near)

    def forward(j):
        @pl.when(lax.rem(rank, stride) == 0)
        def _():
            owner = lax.div(rank, stride)
            rows = pl.ds(pl.multiple_of(owner * chunk, chunk), chunk)
            total = raw_send[j, rows].astype(F32)
            for peer in peers:
                rs_copy(j, 0, peer).wait_recv()
            for peer in peers:
                total = total + raw_recv[j, peer].astype(F32)
            squares = total[:, 3 * cols : 3 * cols + 1] + total[:, 3 * cols + 1 : 3 * cols + 2]
            inverse = lax.rsqrt(squares / full + EPS)
            high = inverse.astype(BF16).astype(F32)
            lane = lax.broadcasted_iota(jnp.int32, (chunk, HEAD_DIM), 1)
            qkv_buf[j, rows, : 3 * cols] = (total[:, : 3 * cols] * inverse).astype(BF16)
            qkv_buf[j, rows, 3 * cols :] = jnp.where(lane == 0, high, inverse - high).astype(BF16)
            for peer in peers:
                ag_copy(j, owner, peer).start()

        @pl.when(j == first)
        def _():
            scatter(1 - first)
            send_weights(near, False)

        for owner in range(shares):

            @pl.when(rank != owner * stride)
            def _(owner=owner):
                ag_copy(j, owner, rank).wait_recv()

        coded = qkv_buf[j, :, 3 * cols :].astype(F32)
        inverse = coded[:, 0:1] + coded[:, 1:2]
        inv_s[j] = jnp.broadcast_to(inverse, (seq, HEAD_DIM))
        qkv = qkv_buf[j, :, : 3 * cols]
        row = lax.broadcasted_iota(jnp.int32, (seq, seq), 0)
        col = lax.broadcasted_iota(jnp.int32, (seq, seq), 1)
        doc = jnp.broadcast_to(doc_ref[j].astype(F32), (seq, seq))
        allowed = (doc.T == doc) & (col <= row)
        for h in range(heads):
            lo, hi = h * HEAD_DIM, (h + 1) * HEAD_DIM
            query, keys = qkv[:, lo:hi], qkv[:, cols + lo : cols + hi]
            values = qkv[:, 2 * cols + lo : 2 * cols + hi]
            scores = jnp.where(allowed, dot(query, keys, (1, 1)) * scale, NEG)
            expo = jnp.exp(scores - jnp.max(scores, axis=1, keepdims=True))
            probs = expo / jnp.sum(expo, axis=1, keepdims=True)
            probs_s[j, h] = probs
            right_s[j, :, 3 * cols + lo : 3 * cols + hi] = dot(probs.astype(BF16), values).astype(BF16)

        @pl.when(j != first)
        def _():
            left_s[0] = scaled_buf[...].T
            gram_s[...] = dot(scaled_buf[...], scaled_buf[...], (1, 1))

    def event(j):
        at_end = me == j * last
        at_start = me == (1 - j) * last
        going = jnp.logical_not(at_end)
        nxt = me + 2 * j - 1

        @pl.when(going & (j != near))
        def _():
            crossing(j)

        def arrive(c):
            @pl.when(jnp.logical_not(at_start))
            def _():
                u_copy(j, me, c).wait_recv()

            @pl.when(going)
            def _():
                part = slice(c * piece, (c + 1) * piece)
                term = dot(u_buf[j, :, part], wn_buf[j, part])
                ahead[...] = term if c == 0 else ahead[...] + term

        for c in range(pieces - 1):
            arrive(c)
        for slot in range(n_tensor):

            @pl.when(jnp.logical_not(at_start & (rank == slot)))
            def _(slot=slot):
                dm_copy(j, me, slot, slot).wait_recv()

        total = dm_recv[j, 0].astype(F32)
        for slot in range(1, n_tensor):
            total = total + dm_recv[j, slot].astype(F32)
        dmixed = total.astype(BF16)
        inverse = inv_s[j][:, :1]
        stat = jnp.zeros((seq, 1), F32)
        for h in range(heads):
            lo, hi = h * HEAD_DIM, (h + 1) * HEAD_DIM
            query, keys = qkv_buf[j, :, lo:hi], qkv_buf[j, :, cols + lo : cols + hi]
            values = qkv_buf[j, :, 2 * cols + lo : 2 * cols + hi]
            mixed = right_s[j, :, 3 * cols + lo : 3 * cols + hi]
            probs = probs_s[j, h]
            upper = dmixed[:, lo:hi]
            dprobs = dot(upper, values, (1, 1))
            delta = jnp.sum(upper.astype(F32) * mixed.astype(F32), axis=1, keepdims=True)
            dscores = (probs * (dprobs - delta) * scale).astype(BF16)
            grads = (
                dot(dscores, keys),
                dot(dscores, query, (0, 0)),
                dot(probs.astype(BF16), upper, (0, 0)),
            )
            for i, (grad, saved) in enumerate(zip(grads, (query, keys, values))):
                at = i * cols
                stat = stat + jnp.sum(grad * saved.astype(F32), axis=1, keepdims=True)
                right_s[j, :, at + lo : at + hi] = (grad * inverse).astype(BF16)
        coeff = inverse * inverse * stat / full
        coeff_s[j] = jnp.broadcast_to(coeff, (seq, HEAD_DIM))
        arrive(pieces - 1)

        @pl.when(going)
        def _():
            right = right_s[j, :, : 3 * cols]
            step = ahead[...] + dot(right, cross[j]) - coeff * cross_x[j]
            dm_send[j] = step.astype(BF16)
            for peer in range(n_tensor):
                dm_copy(j, nxt, peer, rank).start()
            for c in range(pieces):
                finish(j, c)
                u_copy(j, nxt, c).start()

    def finish(j, c):
        part = slice(c * piece, (c + 1) * piece)
        coeff = coeff_s[j][:, :1]
        dscaled = None
        for i in range(3):
            term = dot(right_s[j, :, i * cols : (i + 1) * cols], w_buf[i, part], (1, 1))
            dscaled = term if dscaled is None else dscaled + term
        result = (
            u_buf[j, :, part].astype(F32)
            + gain_ref[:, part] * dscaled
            - x_ref[j, :, part].astype(F32) * coeff
        )
        grads_ref[j, :, part] = result.astype(BF16)

    def turn(k, unused):
        swap = jnp.where(early, 1, 0).astype(jnp.int32)
        second_half = k // 2
        other = lax.rem(k, 2)
        which = jnp.where(swap == 1, second_half, other)
        is_event = jnp.where(swap == 1, other, second_half)
        j = lax.rem(first + which, 2)

        @pl.when(is_event == 0)
        def _():
            forward(j)

        @pl.when(is_event == 1)
        def _():
            event(j)

        return unused

    lax.fori_loop(0, 4, turn, 0)

    stacked = jnp.concatenate([u_buf[0], u_buf[1]], axis=0)
    for m in range(4):
        gram = gram_s[...] if m < 3 else dot(stacked, stacked, (1, 1))
        for h in range(heads):
            lo = m * cols + h * HEAD_DIM
            both = jnp.concatenate(
                [right_s[0, :, lo : lo + HEAD_DIM], right_s[1, :, lo : lo + HEAD_DIM]], axis=0
            )
            sums = jnp.sum(gram * dot(both, both, (1, 1)), axis=0, keepdims=True)
            tot_send[m * heads + h : m * heads + h + 1, :] = sums
    tot_recv[rank] = tot_send[...]
    for peer in peers:
        tot_copy(peer, rank).start()

    @pl.when(outer)
    def _():
        for c in range(pieces):
            finish(1 - first, c)

    left_s[1] = stacked.T
    load_moment.wait()
    for m in range(4):
        both = jnp.concatenate(
            [right_s[0, :, m * cols : (m + 1) * cols], right_s[1, :, m * cols : (m + 1) * cols]], axis=0
        )
        for c in range(pieces):
            part = slice(c * piece, (c + 1) * piece)
            grads = dot(left_s[m // 3, part], both)
            moment_ref[m, part] = BETA_ONE * moment_ref[m, part] + (1.0 - BETA_ONE) * grads
    for peer in peers:
        tot_copy(peer, peer).wait_recv()
    total = tot_recv[0]
    for slot in range(1, n_tensor):
        total = total + tot_recv[slot]
    totals = jnp.sum(total, axis=1, keepdims=True)
    for m in range(4):
        for h in range(heads):
            at = m * heads + h
            second = BETA_TWO * second_ref[h : h + 1, m : m + 1] + (1.0 - BETA_TWO) * totals[
                at : at + 1
            ] / (full * HEAD_DIM)
            second_out_ref[h : h + 1, m : m + 1] = second
            denom = jnp.sqrt(second / CORRECT_TWO) + ADAM_EPS
            scale_ref[at : at + 1, :] = jnp.broadcast_to(1.0 / (denom * CORRECT_ONE), (1, HEAD_DIM))

    for j in range(2):
        for owner in range(shares):

            @pl.when(rank != owner * stride)
            def _(j=j, owner=owner):
                rs_copy(j, owner, rank).wait_send()

        @pl.when(lax.rem(rank, stride) == 0)
        def _(j=j):
            for peer in peers:
                ag_copy(j, lax.div(rank, stride), peer).wait_send()

    for peer in peers:
        tot_copy(peer, rank).wait_send()
    for j, start in ((0, last), (1, 0)):

        @pl.when(me == start)
        def _(j=j):
            for peer in peers:
                start_copy(j, peer, rank).wait_send()

        @pl.when(me != j * last)
        def _(j=j):
            nxt = me + 2 * j - 1
            for peer in range(n_tensor):
                dm_copy(j, nxt, peer, rank).wait_send()
            for c in range(pieces):
                u_copy(j, nxt, c).wait_send()

        @pl.when(me != (1 - j) * last)
        def _(j=j):
            for c in range(pieces):
                wn_copy(j, me + 1 - 2 * j, c).wait_send()


def update_kernel(
    moment_ref, scale_ref, grads_ref, second_ref, out_hbm, grads_hbm, second_out_ref, out_buf, out_sem, grads_sem
):
    count, width, cols = moment_ref.shape
    heads = cols // HEAD_DIM
    pieces = 2 if width % 256 == 0 else 1
    piece = width // pieces
    copy_grads = pltpu.make_async_copy(grads_ref, grads_hbm, grads_sem)
    copy_grads.start()
    copies = []
    for m in range(count):
        row = jnp.concatenate([scale_ref[m * heads + h : m * heads + h + 1] for h in range(heads)], axis=1)
        for c in range(pieces):
            part = pl.ds(c * piece, piece)
            out_buf[m, part] = (moment_ref[m, part] * row).astype(BF16)
            copy = pltpu.make_async_copy(out_buf.at[m, part], out_hbm.at[m, part], out_sem.at[m, c])
            copy.start()
            copies.append(copy)
    second_out_ref[...] = second_ref[...]
    for copy in copies:
        copy.wait()
    copy_grads.wait()


def on_device(
    n_pipe,
    n_tensor,
    section_inputs,
    cotangent,
    documents,
    gain,
    w_query,
    w_key,
    w_value,
    w_out,
    first_moment,
    second_moment,
):
    x = jnp.swapaxes(section_inputs[0], 1, 2)
    cot = jnp.swapaxes(cotangent, 1, 2)
    _, seq, width = x.shape
    cols = w_query.shape[2]
    heads = cols // HEAD_DIM
    rows = 4 * heads
    raw_cols = 3 * cols + HEAD_DIM
    shares = min(n_tensor, seq // 16)
    pieces = 2 if width % 256 == 0 else 1
    vmem = pl.BlockSpec(memory_space=pltpu.VMEM)
    hbm = pl.BlockSpec(memory_space=pltpu.HBM)
    dma = pltpu.SemaphoreType.DMA
    held = functools.partial(pltpu.with_memory_space_constraint, memory_space=pltpu.HBM)
    grads, moment, second, scales = pl.pallas_call(
        functools.partial(relay_kernel, n_pipe, n_tensor),
        name="relay",
        out_shape=(
            pltpu.VMEM((2, seq, width), BF16),
            pltpu.VMEM((4, width, cols), F32),
            pltpu.VMEM((heads, 4), F32),
            pltpu.VMEM((rows, HEAD_DIM), F32),
        ),
        in_specs=[hbm, hbm, vmem] + [hbm] * 6 + [vmem],
        out_specs=(vmem,) * 4,
        scratch_shapes=[
            pltpu.VMEM((2, seq, width), BF16),
            pltpu.VMEM((1, width), F32),
            pltpu.VMEM((4, width, cols), BF16),
            pltpu.VMEM((2, seq, width), BF16),
            pltpu.VMEM((2, width, cols), BF16),
            pltpu.VMEM((2, seq, raw_cols), BF16),
            pltpu.VMEM((2, n_tensor, seq // shares, raw_cols), BF16),
            pltpu.VMEM((2, seq, raw_cols), BF16),
            pltpu.VMEM((seq, cols), BF16),
            pltpu.VMEM((2, seq, cols), BF16),
            pltpu.VMEM((2, n_tensor, seq, cols), BF16),
            pltpu.VMEM((2, 3 * cols, cols), BF16),
            pltpu.VMEM((2, seq, cols), F32),
            pltpu.VMEM((seq, cols), F32),
            pltpu.VMEM((2, seq, 4 * cols), BF16),
            pltpu.VMEM((2, heads, seq, seq), F32),
            pltpu.VMEM((2, seq, HEAD_DIM), F32),
            pltpu.VMEM((2, seq, HEAD_DIM), F32),
            pltpu.VMEM((2 * seq, width), BF16),
            pltpu.VMEM((2, width, 2 * seq), BF16),
            pltpu.VMEM((2 * seq, 2 * seq), F32),
            pltpu.VMEM((rows, 2 * seq), F32),
            pltpu.VMEM((n_tensor, rows, 2 * seq), F32),
            dma((2, shares)),
            dma((2, n_tensor)),
            dma((2, n_tensor)),
            dma((2, shares)),
            dma((n_tensor,)),
            dma((2, n_tensor)),
            dma((2, n_tensor)),
            dma((2, pieces)),
            dma((2, pieces)),
            dma((2, pieces)),
            dma((2, pieces)),
            dma((n_tensor,)),
            dma((n_tensor,)),
            dma((6,)),
            dma,
            dma,
        ],
        compiler_params=pltpu.CompilerParams(
            collective_id=0, has_side_effects=True, vmem_limit_bytes=48 * 2**20
        ),
    )(
        held(x),
        held(cot),
        documents[:, None, :],
        held(gain),
        held(w_query[0]),
        held(w_key[0]),
        held(w_value[0]),
        held(w_out[0]),
        held(first_moment[0]),
        jnp.swapaxes(second_moment[0], 0, 1),
    )
    update, grads, second = pl.pallas_call(
        update_kernel,
        name="update",
        out_shape=(
            jax.ShapeDtypeStruct((4, width, cols), BF16),
            jax.ShapeDtypeStruct((2, seq, width), BF16),
            jax.ShapeDtypeStruct((heads, 4), F32),
        ),
        in_specs=[vmem] * 4,
        out_specs=(hbm, hbm, vmem),
        scratch_shapes=[
            pltpu.VMEM((4, width, cols), BF16),
            dma((4, pieces)),
            dma,
        ],
        compiler_params=pltpu.CompilerParams(vmem_limit_bytes=32 * 2**20),
    )(moment, scales, grads, second)
    return (
        jnp.swapaxes(grads, 1, 2)[None],
        update[None],
        jnp.swapaxes(second, 0, 1)[None],
    )


def solution(mesh):
    placed = (
        P("pipe", None, "tensor", None),
        P(None, "tensor", None),
        P(),
        P("pipe", "tensor"),
        P("pipe", "tensor", None),
        P("pipe", "tensor", None),
        P("pipe", "tensor", None),
        P("pipe", "tensor", None),
        P("pipe", None, "tensor", None),
        P("pipe", None, None),
    )
    return jax.shard_map(
        functools.partial(on_device, mesh.shape["pipe"], mesh.shape["tensor"]),
        mesh=mesh,
        in_specs=placed,
        out_specs=(
            P("pipe", None, "tensor", None),
            P("pipe", None, "tensor", None),
            P("pipe", None, None),
        ),
        check_vma=False,
    )
```
